32 devices in a mesh: aa: 4 (over x, core), ba: 4 (over z), col: 2 (over y).
Axes of the slice: x: 2, y: 2, z: 4, core: 2. Of those that a mesh axis runs over, the one named last changes fastest.
Arguments:
- tokens: bfloat16 [64, 32, 64, 1024], P('aa', 'ba', 'col'), may hold values from -6 to 6
- norm_gain: float32 [1024], replicated, may hold values from 0.1 to 1.9
- in_weight: bfloat16 [1024, 3072], replicated, may hold values from -0.1875 to 0.1875
- skip_gain: float32 [1024], replicated, may hold values from 0.5 to 1.5
- spectrum_filter: bfloat16 [2, 64, 32, 64, 1024], P(None, ('ba', 'col'), None, None, 'aa'), may hold values from -4 to 4
- out_weight: bfloat16 [1024, 1024], replicated, may hold values from -0.1875 to 0.1875
Outputs:
- layer_out: bfloat16 [64, 32, 64, 1024], P('aa', 'ba', 'col')
The draws below stay inside these ranges and needn't reach their ends.
All inputs are finite; a program needn't handle non-finite values.
Results may differ from the reference program's by a relative error of at most 0.014.
Values may be sent and summed in bfloat16 or wider, within the bound.
A program may use at most 256 MiB of HBM per device.

```python
import math
import jax
import jax.numpy as jnp
from jax import lax

LA = 64
LB = 32
LC = 64
D = 1024


def steps_of(own_key, extent, split, smallest, largest):
    def one(dim, shards_of):
        heights = jax.random.uniform(jax.random.fold_in(jax.random.fold_in(own_key, 6), dim), (shards_of,), jnp.float32, smallest / len(split), largest / len(split))
        return jnp.repeat(jnp.exp(heights), extent[dim] // shards_of).reshape((-1,) + (1,) * (len(extent) - dim - 1))

    gain = one(*split[0])
    for cut in split[1:]:
        gain = gain * one(*cut)
    return gain


def centred(stream_key, shape, width, limit, pieces=(), kind=jnp.bfloat16):
    values = width * jax.random.normal(stream_key, shape, jnp.float32)
    if pieces:
        values = values * steps_of(stream_key, shape, pieces, -0.22, 0.18)
    return jnp.clip(values, -limit, limit).astype(kind)


def setup_inputs(seed: int = 0) -> dict:
    splits = jax.random.split(jax.random.key(seed), 7)
    return {
        "tokens": centred(splits[0], (LA, LB, LC, D), 1.0, 6.0, ((0, 4), (1, 4), (2, 2))),
        "norm_gain": jnp.clip(1.0 + 0.18 * jax.random.normal(splits[1], (D,), jnp.float32), 0.1, 1.9),
        "in_weight": centred(splits[2], (D, 3 * D), D ** -0.5, 0.1875),
        "skip_gain": jnp.clip(jax.random.uniform(splits[3], (D,), jnp.float32, 0.5, 1.5), 0.5, 1.5),
        "spectrum_filter": centred(splits[4], (2, LA, LB, LC, D), 0.7, 4.0, ((1, 8), (4, 4))),
        "out_weight": centred(splits[5], (D, D), D ** -0.5, 0.1875),
    }


EPSILON = 1e-06

def dft_tables(length):
    counter = jnp.arange(length, dtype=jnp.int32)
    product = counter[:, None] * counter[None, :] % length
    angle = 2.0 * math.pi / length * product.astype(jnp.float32)
    factor = 1.0 / math.sqrt(length)
    cos_table = (jnp.cos(angle) * factor).astype(jnp.bfloat16).astype(jnp.float32)
    sin_table = (jnp.sin(angle) * factor).astype(jnp.bfloat16).astype(jnp.float32)
    return (cos_table, sin_table)

def phase_pair(integer_phase, modulus):
    angle = 2.0 * math.pi / modulus * (integer_phase % modulus).astype(jnp.float32)
    return (jnp.cos(angle), jnp.sin(angle))

def rounded(value):
    return lax.optimization_barrier(value.astype(jnp.bfloat16)).astype(jnp.float32)

def reference(tokens, norm_gain, in_weight, skip_gain, spectrum_filter, out_weight):
    points = LA * LB * LC
    rows = tokens.reshape(LA, LB * LC, D)

    def project(block):
        flat = block.astype(jnp.float32)
        meansq = lax.optimization_barrier(jnp.mean(flat * flat, axis=-1, keepdims=True))
        normed = (flat * lax.rsqrt(meansq + EPSILON) * norm_gain).astype(jnp.bfloat16)
        projected = jnp.dot(normed, in_weight, preferred_element_type=jnp.float32)
        mixed_rows = (projected[:, :D] * projected[:, 2 * D:]).astype(jnp.bfloat16)
        gate_rows = projected[:, D:2 * D].astype(jnp.bfloat16)
        return (mixed_rows, gate_rows)
    mixed, gate = lax.map(project, rows)
    cos_a, sin_a = dft_tables(LA)
    cos_b, sin_b = dft_tables(LB)
    cos_c, sin_c = dft_tables(LC)
    freq_a = jnp.arange(LA, dtype=jnp.int32)
    index_j = jnp.arange(LB, dtype=jnp.int32)
    index_k = jnp.arange(LC, dtype=jnp.int32)
    cos_phi, sin_phi = phase_pair((LC * index_j[None, :, None] + index_k[None, None, :]) * freq_a[:, None, None], points)
    cos_phi = cos_phi[..., None]
    sin_phi = sin_phi[..., None]
    cos_psi, sin_psi = phase_pair(index_j[:, None] * index_k[None, :], LB * LC)
    cos_psi = cos_psi[None, :, :, None]
    sin_psi = sin_psi[None, :, :, None]
    group = 128 if D % 128 == 0 else D
    ngroups = D // group
    mixed_groups = mixed.reshape(LA, LB, LC, ngroups, group).transpose(3, 0, 1, 2, 4)
    filter_groups = spectrum_filter.reshape(2, LA, LB, LC, ngroups, group).transpose(4, 0, 1, 2, 3, 5)

    def spectral(operands):
        block, filt = operands
        source = block.astype(jnp.float32)
        real_part = jnp.einsum('fi,ijkc->fjkc', cos_a, source)
        imag_part = -jnp.einsum('fi,ijkc->fjkc', sin_a, source)
        first_real = rounded(real_part * cos_phi + imag_part * sin_phi)
        first_imag = rounded(imag_part * cos_phi - real_part * sin_phi)
        real_part = jnp.einsum('gj,fjkc->fgkc', cos_b, first_real) + jnp.einsum('gj,fjkc->fgkc', sin_b, first_imag)
        imag_part = jnp.einsum('gj,fjkc->fgkc', cos_b, first_imag) - jnp.einsum('gj,fjkc->fgkc', sin_b, first_real)
        second_real = rounded(real_part * cos_psi + imag_part * sin_psi)
        second_imag = rounded(imag_part * cos_psi - real_part * sin_psi)
        spec_real = jnp.einsum('hk,fgkc->fghc', cos_c, second_real) + jnp.einsum('hk,fgkc->fghc', sin_c, second_imag)
        spec_imag = jnp.einsum('hk,fgkc->fghc', cos_c, second_imag) - jnp.einsum('hk,fgkc->fghc', sin_c, second_real)
        filt_real = filt[0].astype(jnp.float32)
        filt_imag = filt[1].astype(jnp.float32)
        filtered_real = rounded(filt_real * spec_real - filt_imag * spec_imag)
        filtered_imag = rounded(filt_real * spec_imag + filt_imag * spec_real)
        real_part = jnp.einsum('hk,fghc->fgkc', cos_c, filtered_real) - jnp.einsum('hk,fghc->fgkc', sin_c, filtered_imag)
        imag_part = jnp.einsum('hk,fghc->fgkc', cos_c, filtered_imag) + jnp.einsum('hk,fghc->fgkc', sin_c, filtered_real)
        third_real = rounded(real_part * cos_psi - imag_part * sin_psi)
        third_imag = rounded(imag_part * cos_psi + real_part * sin_psi)
        real_part = jnp.einsum('gj,fgkc->fjkc', cos_b, third_real) - jnp.einsum('gj,fgkc->fjkc', sin_b, third_imag)
        imag_part = jnp.einsum('gj,fgkc->fjkc', cos_b, third_imag) + jnp.einsum('gj,fgkc->fjkc', sin_b, third_real)
        back_real = rounded(real_part * cos_phi - imag_part * sin_phi)
        back_imag = rounded(imag_part * cos_phi + real_part * sin_phi)
        result = jnp.einsum('fi,fjkc->ijkc', cos_a, back_real) - jnp.einsum('fi,fjkc->ijkc', sin_a, back_imag)
        return result.astype(jnp.bfloat16)
    conv_groups = lax.map(spectral, (mixed_groups, filter_groups))
    conv = conv_groups.transpose(1, 2, 3, 0, 4).reshape(LA, LB * LC, D)

    def finish(operands):
        conv_rows, gate_rows, mixed_rows = operands
        gated = (gate_rows.astype(jnp.float32) * (conv_rows.astype(jnp.float32) + skip_gain * mixed_rows.astype(jnp.float32))).astype(jnp.bfloat16)
        return jnp.dot(gated, out_weight, preferred_element_type=jnp.float32).astype(jnp.bfloat16)
    layer_out = lax.map(finish, (conv, gate, mixed))
    return layer_out.reshape(LA, LB, LC, D)
```

```python
import math

import jax
import jax.numpy as jnp
from jax import lax
from jax.sharding import PartitionSpec as P

LA = 64
LB = 32
LC = 64
D = 1024


EPSILON = 1e-06


def dft_tables(length):
    counter = jnp.arange(length, dtype=jnp.int32)
    product = counter[:, None] * counter[None, :] % length
    angle = 2.0 * math.pi / length * product.astype(jnp.float32)
    factor = 1.0 / math.sqrt(length)
    return (
        (jnp.cos(angle) * factor).astype(jnp.bfloat16),
        (jnp.sin(angle) * factor).astype(jnp.bfloat16),
    )


def phase_pair(integer_phase, modulus):
    angle = 2.0 * math.pi / modulus * (integer_phase % modulus).astype(jnp.float32)
    return (jnp.cos(angle), jnp.sin(angle))


def contract(form, table, operand):
    return jnp.einsum(form, table, operand, preferred_element_type=jnp.float32)


CHUNKS = 2


def project(normed, weight):
    return jnp.einsum("td,dgc->gtc", normed, weight, preferred_element_type=jnp.float32)


def local(tokens, norm_gain, in_weight, skip_gain, spectrum_filter, out_weight):
    count_aa = lax.axis_size("aa")
    count_ba = lax.axis_size("ba")
    count_col = lax.axis_size("col")
    rows_i = LA // count_aa
    rows_j = LB // count_ba
    rows_k = LC // count_col
    blocks = count_ba * count_col
    freq_local = LA // blocks
    channels = D // count_aa
    points = LA * LB * LC
    flat = tokens.reshape(-1, D).astype(jnp.float32)
    meansq = jnp.mean(flat * flat, axis=-1, keepdims=True)
    normed = (flat * lax.rsqrt(meansq + EPSILON) * norm_gain).astype(jnp.bfloat16)
    width = channels // CHUNKS
    weights = in_weight.reshape(D, 3, count_aa, CHUNKS, width)
    mixed = []
    gate = []
    for q in range(CHUNKS):
        x1 = project(normed, weights[:, 0, :, q])
        v = project(normed, weights[:, 2, :, q])
        mixed.append((x1 * v).astype(jnp.bfloat16))
    arrived = [
        lax.all_to_all(part, "aa", split_axis=0, concat_axis=0, tiled=True) for part in mixed
    ]
    for q in range(CHUNKS):
        gate.append(project(normed, weights[:, 1, :, q]).astype(jnp.bfloat16))
    stages = [
        spectral(
            arrived[q].reshape(LA, rows_j, rows_k, width),
            spectrum_filter[..., q * width : (q + 1) * width],
        )
        for q in range(CHUNKS)
    ]
    first = [None] * CHUNKS
    moved = [None] * CHUNKS
    back = [None] * CHUNKS
    convs = [None] * CHUNKS
    for q in range(CHUNKS):
        first[q] = next(stages[q])
        if q + 1 < CHUNKS:
            first[q], arrived[q + 1] = lax.optimization_barrier((first[q], arrived[q + 1]))
            stages[q + 1] = spectral(
                arrived[q + 1].reshape(LA, rows_j, rows_k, width),
                spectrum_filter[..., (q + 1) * width : (q + 2) * width],
            )
        moved[q] = stages[q].send(first[q])
    for q in range(CHUNKS):
        back[q] = stages[q].send(moved[q])
        if q + 1 < CHUNKS:
            back[q], moved[q + 1] = lax.optimization_barrier((back[q], moved[q + 1]))
        convs[q] = stages[q].send(back[q])
    gated = []
    skips = skip_gain.reshape(count_aa, 1, CHUNKS, width)
    for q in range(CHUNKS):
        conv_part = convs[q]
        conv_part = conv_part.reshape(count_aa, rows_i * rows_j * rows_k, width)
        conv = lax.all_to_all(conv_part, "aa", split_axis=0, concat_axis=0, tiled=True)
        conv = conv.astype(jnp.float32)
        total = conv + skips[:, :, q] * mixed[q].astype(jnp.float32)
        gated.append((gate[q].astype(jnp.float32) * total).astype(jnp.bfloat16))
    joined = jnp.concatenate(gated, axis=-1)
    out_blocks = out_weight.reshape(count_aa, channels, D)
    layer_out = jnp.einsum(
        "gtc,gcd->td", joined, out_blocks, preferred_element_type=jnp.float32
    ).astype(jnp.bfloat16)
    return layer_out.reshape(rows_i, rows_j, rows_k, D)


def spectral(by_rows, spectrum_filter):
    count_ba = lax.axis_size("ba")
    count_col = lax.axis_size("col")
    rows_j = LB // count_ba
    rows_k = LC // count_col
    blocks = count_ba * count_col
    freq_local = LA // blocks
    channels = by_rows.shape[-1]
    points = LA * LB * LC
    cos_a, sin_a = dft_tables(LA)
    real_part = contract("fi,ijkx->fjkx", cos_a, by_rows)
    imag_part = -contract("fi,ijkx->fjkx", sin_a, by_rows)
    j_global = lax.axis_index("ba") * rows_j + jnp.arange(rows_j, dtype=jnp.int32)
    k_global = lax.axis_index("col") * rows_k + jnp.arange(rows_k, dtype=jnp.int32)
    freq_all = jnp.arange(LA, dtype=jnp.int32)
    cos_phi, sin_phi = phase_pair(
        (LC * j_global[None, :, None] + k_global[None, None, :]) * freq_all[:, None, None], points
    )
    cos_phi = cos_phi[..., None]
    sin_phi = sin_phi[..., None]
    first = jnp.stack(
        [real_part * cos_phi + imag_part * sin_phi, imag_part * cos_phi - real_part * sin_phi]
    ).astype(jnp.bfloat16)
    first = yield first
    shaped = first.reshape(2, blocks, 1, freq_local, rows_j, rows_k, channels)
    moved = lax.all_to_all(shaped, ("ba", "col"), split_axis=1, concat_axis=2, tiled=True)
    moved = yield moved
    moved = moved.reshape(2, count_ba, count_col, freq_local, rows_j, rows_k, channels)
    cos_b, sin_b = dft_tables(LB)
    cos_b = cos_b.reshape(LB, count_ba, rows_j)
    sin_b = sin_b.reshape(LB, count_ba, rows_j)
    moved_real = moved[0]
    moved_imag = moved[1]
    form_two = "gbj,bcfjkx->fgckx"
    real_part = contract(form_two, cos_b, moved_real) + contract(form_two, sin_b, moved_imag)
    imag_part = contract(form_two, cos_b, moved_imag) - contract(form_two, sin_b, moved_real)
    index_g = jnp.arange(LB, dtype=jnp.int32)
    index_k = jnp.arange(LC, dtype=jnp.int32)
    cos_psi, sin_psi = phase_pair(index_g[:, None] * index_k[None, :], LB * LC)
    cos_psi = cos_psi.reshape(1, LB, count_col, rows_k, 1)
    sin_psi = sin_psi.reshape(1, LB, count_col, rows_k, 1)
    second_real = (real_part * cos_psi + imag_part * sin_psi).astype(jnp.bfloat16)
    second_imag = (imag_part * cos_psi - real_part * sin_psi).astype(jnp.bfloat16)
    cos_c, sin_c = dft_tables(LC)
    cos_c = cos_c.reshape(LC, count_col, rows_k)
    sin_c = sin_c.reshape(LC, count_col, rows_k)
    form_three = "hck,fgckx->fghx"
    spec_real = contract(form_three, cos_c, second_real) + contract(form_three, sin_c, second_imag)
    spec_imag = contract(form_three, cos_c, second_imag) - contract(form_three, sin_c, second_real)
    filt_real = spectrum_filter[0].astype(jnp.float32)
    filt_imag = spectrum_filter[1].astype(jnp.float32)
    filtered_real = (filt_real * spec_real - filt_imag * spec_imag).astype(jnp.bfloat16)
    filtered_imag = (filt_real * spec_imag + filt_imag * spec_real).astype(jnp.bfloat16)
    form_back_three = "hck,fghx->fgckx"
    real_part = contract(form_back_three, cos_c, filtered_real) - contract(
        form_back_three, sin_c, filtered_imag
    )
    imag_part = contract(form_back_three, cos_c, filtered_imag) + contract(
        form_back_three, sin_c, filtered_real
    )
    third_real = (real_part * cos_psi - imag_part * sin_psi).astype(jnp.bfloat16)
    third_imag = (imag_part * cos_psi + real_part * sin_psi).astype(jnp.bfloat16)
    form_back_two = "gbj,fgckx->bcfjkx"
    real_part = contract(form_back_two, cos_b, third_real) - contract(
        form_back_two, sin_b, third_imag
    )
    imag_part = contract(form_back_two, cos_b, third_imag) + contract(
        form_back_two, sin_b, third_real
    )
    slot = lax.axis_index("ba") * count_col + lax.axis_index("col")
    freq_global = slot * freq_local + jnp.arange(freq_local, dtype=jnp.int32)
    j_all = jnp.arange(LB, dtype=jnp.int32).reshape(count_ba, rows_j)
    k_all = jnp.arange(LC, dtype=jnp.int32).reshape(count_col, rows_k)
    integer_phase = (
        LC * j_all[:, None, None, :, None] + k_all[None, :, None, None, :]
    ) * freq_global[None, None, :, None, None]
    cos_back, sin_back = phase_pair(integer_phase, points)
    cos_back = cos_back[..., None]
    sin_back = sin_back[..., None]
    back_second = jnp.stack(
        [real_part * cos_back - imag_part * sin_back, imag_part * cos_back + real_part * sin_back]
    ).astype(jnp.bfloat16)
    back_second = yield back_second
    shaped = back_second.reshape(2, 1, blocks, freq_local, rows_j, rows_k, channels)
    returned = lax.all_to_all(shaped, ("ba", "col"), split_axis=2, concat_axis=1, tiled=True)
    returned = returned.reshape(2, LA, rows_j, rows_k, channels)
    conv_part = (
        contract("fi,fjkx->ijkx", cos_a, returned[0])
        - contract("fi,fjkx->ijkx", sin_a, returned[1])
    ).astype(jnp.bfloat16)
    yield conv_part


def solution(mesh):
    in_specs = (
        P("aa", "ba", "col", None),
        P(),
        P(),
        P(),
        P(None, ("ba", "col"), None, None, "aa"),
        P(),
    )
    out_specs = P("aa", "ba", "col", None)
    return jax.shard_map(local, mesh=mesh, in_specs=in_specs, out_specs=out_specs, check_vma=False)
```
